32 devices in a mesh: ctx: 8 (over z, y), head: 4 (over x, core).
Axes of the slice: x: 2, y: 2, z: 4, core: 2. Of those that a mesh axis runs over, the one named last changes fastest.
Arguments:
- hidden_in: bfloat16 [4096, 3584], P('ctx', 'head'), may hold values from -60 to 60, as said below
- w_query: bfloat16 [3584, 2048], P(None, 'head'), may hold values from -0.09375 to 0.09375
- w_key: bfloat16 [3584, 512], P(None, 'head'), may hold values from -0.09375 to 0.09375
- w_value: bfloat16 [3584, 512], P(None, 'head'), may hold values from -0.09375 to 0.09375
- w_output: bfloat16 [2048, 3584], P('head'), may hold values from -0.125 to 0.125
- vertical: int32 [4, 4, 4], P('head'), may hold values from 0 to 31
- slash_offsets: int32 [4, 4, 4], P('head'), may hold values from 1 to 31
Outputs:
- attn_out: bfloat16 [4096, 3584], P(('ctx', 'head'))
The draws below stay inside these ranges and needn't reach their ends.
Inputs may be any that keep to these rules, and one draw needn't show every extreme that they name: `hidden_in`: hidden states of order one, with some rows far larger in some draws.
All inputs are finite; a program needn't handle non-finite values.
Results may differ from the reference program's by a relative error of at most 0.012.
The reference program's roundings to bfloat16 on the way (of `weights` and `context`) count: a program that leaves them out, or rounds other values in their place, can miss the bound.
Values may be sent and summed in bfloat16 or wider, within the bound.
A program may use at most 128 MiB of HBM per device.

```python
import math
import jax
import jax.numpy as jnp
from jax import lax

D = 3584
HD = 128
KVH = 4
QH = 4
BS = 128
NV = 4
NS = 4
TOKENS = 4096
NB = 32


def draw_hidden_in(key, part):
    first_key = jax.random.fold_in(key, 11)
    values = jnp.clip(jax.random.normal(first_key, (TOKENS, D), jnp.float32), -4.0, 4.0)
    return values.astype(jnp.bfloat16)


def with_ends(drawn, own_key, least, top_value):
    extent = drawn.shape
    index_at = [jax.random.randint(jax.random.fold_in(own_key, axis), (), 0, extent[axis]) for axis in range(len(extent))]
    drawn = drawn.at[tuple(index_at)].set(least)
    longest = extent.index(max(extent))
    index_at[longest] = (index_at[longest] + 1) % extent[longest]
    return drawn.at[tuple(index_at)].set(top_value)


def block_levels(key, extent, cuts, smallest, largest):
    gain = 1.0
    for dim, parts in cuts:
        heights = jax.random.uniform(jax.random.fold_in(jax.random.fold_in(key, 6), dim), (parts,), jnp.float32, smallest / len(cuts), largest / len(cuts))
        gain = gain * jnp.repeat(jnp.exp(heights), extent[dim] // parts).reshape((-1,) + (1,) * (len(extent) - 1 - dim))
    return gain


def noise(key, extent, deviation, limit, pieces=(), held_as=jnp.bfloat16):
    factor_of = block_levels(key, extent, pieces, -0.22, 0.18) if pieces else 1.0
    entries = jax.random.normal(key, extent, jnp.float32) * deviation * factor_of
    return jnp.minimum(jnp.maximum(entries, -limit), limit).astype(held_as)


def setup_inputs(seed: int = 0) -> dict:
    streams_of = jax.random.split(jax.random.key(seed), 8)
    hidden_in = draw_hidden_in(jax.random.fold_in(streams_of[7], 71), 0)
    w_query = noise(streams_of[1], (D, KVH * QH * HD), D ** -0.5, 0.09375, ((1, 4),))
    w_key = noise(streams_of[2], (D, KVH * HD), D ** -0.5, 0.09375, ((1, 4),))
    w_value = noise(streams_of[3], (D, KVH * HD), D ** -0.5, 0.09375, ((1, 4),))
    w_output = noise(streams_of[4], (KVH * QH * HD, D), (KVH * QH * HD) ** -0.5, 0.125, ((0, 4),))
    vertical = with_ends(jax.random.randint(streams_of[5], (KVH, QH, NV), 0, NB), jax.random.fold_in(streams_of[5], 1), 0, NB - 1).astype(jnp.int32)
    slash_offsets = with_ends(jax.random.randint(streams_of[6], (KVH, QH, NS), 1, NB), jax.random.fold_in(streams_of[6], 1), 1, NB - 1).astype(jnp.int32)
    return dict(hidden_in=hidden_in, w_query=w_query, w_key=w_key, w_value=w_value, w_output=w_output, vertical=vertical, slash_offsets=slash_offsets)


THETA = 10000000.0

def rotate(values, positions):
    half = values.shape[-1] // 2
    freq = jnp.exp(-(jnp.arange(half, dtype=jnp.float32) * 2.0 / values.shape[-1]) * math.log(THETA))
    angle = positions.astype(jnp.float32)[:, None, None] * freq[None, None, :]
    cosine = jnp.cos(angle)
    sine = jnp.sin(angle)
    first = values[..., :half]
    second = values[..., half:]
    return jnp.concatenate([first * cosine - second * sine, second * cosine + first * sine], axis=-1)

def slot_table(qblocks, columns, offsets):
    lead = columns.shape[:-1]
    count = qblocks.shape[0]
    diag = jnp.broadcast_to(qblocks.astype(jnp.int32)[:, None], lead + (count, 1))
    back = qblocks.astype(jnp.int32)[:, None] - offsets[..., None, :]
    upright = jnp.broadcast_to(columns[..., None, :], lead + (count, columns.shape[-1]))
    slots = jnp.concatenate([diag, back, upright], axis=-1).astype(jnp.int32)
    width = slots.shape[-1]
    same = slots[..., :, None] == slots[..., None, :]
    lower = jnp.tril(jnp.ones((width, width), dtype=bool), -1)
    repeated = jnp.any(same & lower, axis=-1)
    valid = (slots >= 0) & (slots <= qblocks.astype(jnp.int32)[:, None]) & jnp.logical_not(repeated)
    return (jnp.maximum(slots, 0).astype(jnp.int32), valid)

def sparse_attend(query, key_blocks, value_blocks, qblocks, columns, offsets):
    heads, count, block, head_dim = query.shape
    slots, valid = slot_table(qblocks, columns, offsets)
    width = slots.shape[-1]
    picked_k = key_blocks[slots].reshape(heads, count, width * block, head_dim)
    picked_v = value_blocks[slots].reshape(heads, count, width * block, head_dim)
    scores = jnp.einsum('hbqd,hbkd->hbqk', query.astype(jnp.float32), picked_k.astype(jnp.float32)) / math.sqrt(head_dim)
    inner = jnp.arange(block, dtype=jnp.int32)
    qpos = qblocks.astype(jnp.int32)[:, None] * block + inner[None, :]
    kpos = (slots[..., None] * block + inner).reshape(heads, count, width * block)
    live = jnp.broadcast_to(valid[..., None], (heads, count, width, block)).reshape(heads, count, width * block)
    allowed = live[:, :, None, :] & (kpos[:, :, None, :] <= qpos[None, :, :, None])
    masked = jnp.where(allowed, scores, jnp.float32(-1e+30))
    top = lax.optimization_barrier(jnp.max(masked, axis=-1, keepdims=True))
    raw = jnp.where(allowed, jnp.exp(masked - top), jnp.float32(0.0))
    total = lax.optimization_barrier(jnp.sum(raw, axis=-1, keepdims=True))
    weights = raw.astype(jnp.bfloat16)
    summed = jnp.einsum('hbqk,hbkd->hbqd', weights.astype(jnp.float32), picked_v.astype(jnp.float32))
    return (summed / total).astype(jnp.bfloat16)

def reference(hidden_in, w_query, w_key, w_value, w_output, vertical, slash_offsets):
    tokens = hidden_in.shape[0]
    positions = jnp.arange(tokens, dtype=jnp.int32)
    proj_q = jnp.dot(hidden_in, w_query, preferred_element_type=jnp.float32).reshape(tokens, KVH * QH, HD)
    proj_k = jnp.dot(hidden_in, w_key, preferred_element_type=jnp.float32).reshape(tokens, KVH, HD)
    proj_v = jnp.dot(hidden_in, w_value, preferred_element_type=jnp.float32).reshape(tokens, KVH, HD)
    query = rotate(proj_q, positions).astype(jnp.bfloat16)
    keys = rotate(proj_k, positions).astype(jnp.bfloat16)
    values = proj_v.astype(jnp.bfloat16)
    key_blocks = keys.reshape(NB, BS, KVH, HD).transpose(2, 0, 1, 3)
    value_blocks = values.reshape(NB, BS, KVH, HD).transpose(2, 0, 1, 3)
    query_blocks = query.reshape(NB, BS, KVH, QH, HD).transpose(0, 2, 3, 1, 4)

    def one_block(inputs):
        block_index, qpart = inputs
        qblocks = jnp.reshape(block_index, (1,)).astype(jnp.int32)

        def per_group(qgroup, kgroup, vgroup, columns, offsets):
            return sparse_attend(qgroup[:, None], kgroup, vgroup, qblocks, columns, offsets)
        return jax.vmap(per_group)(qpart, key_blocks, value_blocks, vertical, slash_offsets)
    outputs = lax.map(one_block, (jnp.arange(NB, dtype=jnp.int32), query_blocks))
    context = outputs[:, :, :, 0].transpose(0, 3, 1, 2, 4).reshape(tokens, KVH * QH * HD)
    return jnp.dot(context, w_output, preferred_element_type=jnp.float32).astype(jnp.bfloat16)
```

```python
import functools
import math

import jax
import jax.numpy as jnp
from jax import lax
from jax.experimental import pallas as pl
from jax.experimental.pallas import tpu as pltpu
from jax.sharding import PartitionSpec as P

BS = 128
PIECE = 64
AHEAD = 1
THETA = 10000000.0
MESH = pl.DeviceIdType.MESH
F32 = jnp.float32
BF16 = jnp.bfloat16


def rope_rates(head_dim):
    lane = lax.broadcasted_iota(jnp.int32, (1, head_dim), 1)
    j = jnp.where(lane < head_dim // 2, lane, lane - head_dim // 2).astype(F32)
    return jnp.exp(-(j * 2.0 / head_dim) * math.log(THETA))


def kernel(
    nctx, nhead,
    vert, slash, hid, wq, wk, wv, wo,
    out,
    w_s, wo_s, mate_x, far_x, fwd_x, acc, q_s, kv, part_m, part_x, in_m, in_x, ctx_s, cos, sin, hid_s,
    wsem, ms, mr, fs, fr, gs, gr, cs, cr, ys, yr, pms, pmr, pxs, pxr,
):
    i, h = lax.axis_index("ctx"), lax.axis_index("head")
    o, p = i // 2, i % 2
    outer = nctx // 2
    pair, c0 = h // 2, h % 2
    pairs = nhead // 2
    hmate = h + 1 - 2 * c0
    ymate = i + 1 - 2 * p
    has_next, has_prev = o < outer - 1, o > 0
    rows = hid.shape[0]
    nchunk = rows // PIECE
    per = BS // PIECE
    hd = cos.shape[1]
    qh = q_s.shape[1] // hd
    ntile, tn = part_m.shape[1], part_m.shape[3]

    def far(d):
        return lax.rem(pair + d, pairs) * 2 + c0

    qw = wq.shape[2]
    loads = [
        pltpu.make_async_copy(wq, w_s.at[:, :, pl.ds(0, qw)], wsem.at[0]),
        pltpu.make_async_copy(wk, w_s.at[:, :, pl.ds(qw, hd)], wsem.at[1]),
        pltpu.make_async_copy(wv, w_s.at[:, :, pl.ds(qw + hd, hd)], wsem.at[2]),
        pltpu.make_async_copy(wo, wo_s, wsem.at[3]),
    ]
    own = pltpu.make_async_copy(hid, hid_s, wsem.at[4])
    own.start()
    for load in loads:
        load.start()

    barrier = pltpu.get_barrier_semaphore()

    def greet(where):
        pl.semaphore_signal(barrier, inc=1, device_id=where, device_id_type=MESH)

    greet({"head": hmate})
    for d in range(1, pairs):
        greet({"head": far(d)})
    greet({"ctx": ymate})

    @pl.when(has_next)
    def _():
        greet({"ctx": i + 2})

    @pl.when(has_prev)
    def _():
        greet({"ctx": i - 2})

    pl.semaphore_wait(
        barrier, pairs + 1 + jnp.where(has_next, 1, 0) + jnp.where(has_prev, 1, 0)
    )

    def remote(src, dst, send, recv, where):
        return pltpu.make_async_remote_copy(
            src_ref=src, dst_ref=dst, send_sem=send, recv_sem=recv,
            device_id=where, device_id_type=MESH,
        )

    def far_copy(d, c):
        return remote(
            hid.at[pl.ds(c * PIECE, PIECE), :], far_x.at[d - 1, c],
            fs.at[d - 1, c], fr.at[d - 1, c], {"head": far(d)},
        )

    def fwd_copy(d, c):
        return remote(
            far_x.at[d - 1, c], fwd_x.at[d - 1, c],
            gs.at[d - 1, c], gr.at[d - 1, c], {"head": hmate},
        )

    mate_copy = remote(hid, mate_x, ms.at[0], mr.at[0], {"head": hmate})
    for c in range(nchunk):
        for d in range(1, pairs):
            far_copy(d, c).start()
    mate_copy.start()

    def next_copy(c, so):
        block = kv.at[(so * 2 + p) * nchunk + c]
        return remote(block, block, cs.at[c, so], cr.at[c, so], {"ctx": i + 2})

    def side_copy(c, so, col):
        block = kv.at[(so * 2 + col) * nchunk + c]
        return remote(block, block, ys.at[c, so], yr.at[c, so], {"ctx": ymate})

    def relay(c, so):
        next_copy(c, so).wait_recv()

        @pl.when(has_next)
        def _():
            next_copy(c, so).start()

        side_copy(c, so, p).start()

    rates = rope_rates(hd)

    def table(c, carry):
        part = pl.ds(pl.multiple_of(c * PIECE, PIECE), PIECE)
        spot = lax.broadcasted_iota(jnp.int32, (PIECE, hd), 0) + (i * rows + c * PIECE)
        angle = spot.astype(F32) * rates
        lane = lax.broadcasted_iota(jnp.int32, (PIECE, hd), 1)
        sine = jnp.sin(angle)
        cos[part, :] = jnp.cos(angle)
        sin[part, :] = jnp.where(lane < hd // 2, -sine, sine)
        return carry

    lax.fori_loop(0, nchunk, table, 0)
    own.wait()
    for load in loads[:3]:
        load.wait()
    wide = w_s.shape[2]
    step = 256 if wide % 256 == 0 else 128

    def own_cols(t, carry):
        cols = pl.ds(pl.multiple_of(t * step, step), step)
        acc[:, cols] = jnp.dot(hid_s[...], w_s[h, :, cols], preferred_element_type=F32)
        return carry

    lax.fori_loop(0, wide // step, own_cols, 0)
    mate_copy.wait_recv()

    def mate_cols(t, carry):
        cols = pl.ds(pl.multiple_of(t * step, step), step)
        acc[:, cols] += jnp.dot(mate_x[...], w_s[hmate, :, cols], preferred_element_type=F32)
        return carry

    lax.fori_loop(0, wide // step, mate_cols, 0)

    def project(c):
        part = pl.ds(pl.multiple_of(c * PIECE, PIECE), PIECE)
        for d in range(1, pairs):
            far_copy(d, c).wait_recv()
            fwd_copy(d, c).start()
            src = lax.rem(pair + pairs - d, pairs) * 2
            acc[part, :] += jnp.dot(
                far_x[d - 1, c], w_s[src + c0], preferred_element_type=F32
            )
            fwd_copy(d, c).wait_recv()
            acc[part, :] += jnp.dot(
                fwd_x[d - 1, c], w_s[src + 1 - c0], preferred_element_type=F32
            )
        cosine, sine = cos[part, :], sin[part, :]

        def rope(u):
            return (u * cosine + pltpu.roll(u, hd // 2, 1) * sine).astype(BF16)

        mine = i * nchunk + c
        kv[mine, :, pl.ds(0, hd)] = rope(acc[part, pl.ds(qw, hd)])
        kv[mine, :, pl.ds(hd, hd)] = acc[part, pl.ds(qw + hd, hd)].astype(BF16)

        @pl.when(has_next)
        def _():
            next_copy(c, o).start()

        @pl.when(p == 0)
        def _():
            side_copy(c, o, p).start()

        for g in range(qh):
            q_s[part, pl.ds(g * hd, hd)] = rope(acc[part, pl.ds(g * hd, hd)])

    def turn(t, carry):
        @pl.when(t < nchunk)
        def _():
            project(t)

        for c in range(nchunk):
            s = t - c

            @pl.when((s >= 1) & (s <= o))
            def _():
                relay(c, o - s)

        return carry

    lax.fori_loop(0, nchunk + outer - 1, turn, 0)

    def passed(so, carry):
        for c in range(nchunk):
            side_copy(c, so, 1 - p).wait_recv()
        return carry

    lax.fori_loop(0, o + p, passed, 0)
    loads[3].wait()

    nv, ns = vert.shape[1], slash.shape[1]
    scale = 1.0 / math.sqrt(hd)
    below = lax.broadcasted_iota(jnp.int32, (BS, BS), 1) <= lax.broadcasted_iota(
        jnp.int32, (BS, BS), 0
    )
    low = F32(-1e30)

    def attend(b, into):
        qb = i * (rows // BS) + b
        query_rows = pl.ds(pl.multiple_of(b * BS, BS), BS)

        def held(at, lanes):
            return kv[pl.ds(at * per, per), :, lanes].reshape(BS, hd)

        for g in range(qh):
            slots = [qb]
            live = [None]
            for s in range(ns + nv):
                slot = qb - slash[g, s] if s < ns else vert[g, s - ns]
                ok = (slot >= 0) & (slot < qb)
                for earlier in slots[1:]:
                    ok = ok & (slot != earlier)
                slots.append(slot)
                live.append(ok)
            query = q_s[query_rows, pl.ds(g * hd, hd)]
            at = [s if ok is None else jnp.where(ok, s, qb) for s, ok in zip(slots, live)]
            groups = [[0]] + [[n, n + 1] for n in range(1, len(at) - 1, 2)]
            if len(at) % 2 == 0:
                groups.append([len(at) - 1])
            scores = []
            for group in groups:
                keys = jnp.concatenate([held(at[n], pl.ds(0, hd)) for n in group], axis=0)
                both = lax.dot_general(
                    query, keys, (((1,), (1,)), ((), ())), preferred_element_type=F32
                ) * F32(scale)
                for m, n in enumerate(group):
                    sc = both[:, m * BS:(m + 1) * BS]
                    scores.append(jnp.where(below if n == 0 else live[n], sc, low))
            top = functools.reduce(jnp.maximum, scores)
            top = jnp.max(top, axis=1, keepdims=True)
            total = None
            summed = None
            for group in groups:
                raws = [jnp.exp(scores[n] - top) for n in group]
                for raw in raws:
                    total = raw if total is None else total + raw
                vals = jnp.concatenate([held(at[n], pl.ds(hd, hd)) for n in group], axis=0)
                weights = jnp.concatenate([raw.astype(BF16) for raw in raws], axis=1)
                add = jnp.dot(weights, vals, preferred_element_type=F32)
                summed = add if summed is None else summed + add
            total = jnp.sum(total, axis=1, keepdims=True)
            ctx_s[into, :, pl.ds(g * hd, hd)] = (summed / total).astype(BF16)

    def share(t, of):
        cols = pl.ds(pl.multiple_of(t * tn, tn), tn)
        return jnp.dot(ctx_s[of], wo_s[:, cols], preferred_element_type=F32)

    def to_mate(r, t):
        return remote(
            part_m.at[r, t], in_m.at[r, t], pms.at[r, t], pmr.at[r, t], {"head": hmate}
        )

    def to_far(r, t):
        return remote(
            part_x.at[r, t], in_x.at[r, t], pxs.at[r, t], pxr.at[r, t], {"head": far(r + 1)}
        )

    def give(r, t):
        part_m[r, t] = share(t, 0).astype(BF16)
        to_mate(r, t).start()

    def round_of(r, carry):
        to = lax.rem(pair + r + 1, pairs) * 2
        attend(to + 1 - c0, 0)
        for t in range(AHEAD):
            give(r, t)
        attend(to + c0, 1)

        def tile(t, carry):
            mine = share(t, 1)
            to_mate(r, t).wait_recv()
            part_x[r, t] = (mine + in_m[r, t].astype(F32)).astype(BF16)
            to_far(r, t).start()

            @pl.when(t + AHEAD < ntile)
            def _():
                give(r, t + AHEAD)

            return carry

        lax.fori_loop(0, ntile, tile, 0)
        return carry

    lax.fori_loop(0, pairs - 1, round_of, 0)
    attend(pair * 2 + 1 - c0, 0)

    def give_last(t, carry):
        give(pairs - 1, t)
        return carry

    lax.fori_loop(0, ntile, give_last, 0)
    attend(h, 1)

    def last(t, carry):
        mine = share(t, 1)
        to_mate(pairs - 1, t).wait_recv()
        mine = mine + in_m[pairs - 1, t].astype(F32)
        for r in range(pairs - 1):
            to_far(r, t).wait_recv()
            mine = mine + in_x[r, t].astype(F32)
        out[:, pl.ds(pl.multiple_of(t * tn, tn), tn)] = mine.astype(out.dtype)
        return carry

    lax.fori_loop(0, ntile, last, 0)

    mate_copy.wait_send()
    for c in range(nchunk):
        for d in range(1, pairs):
            far_copy(d, c).wait_send()
            fwd_copy(d, c).wait_send()

    def drain_next(so, carry):
        for c in range(nchunk):
            next_copy(c, so).wait_send()
        return carry

    lax.fori_loop(0, jnp.where(has_next, o + 1, 0), drain_next, 0)

    def drain_side(so, carry):
        for c in range(nchunk):
            side_copy(c, so, p).wait_send()
        return carry

    lax.fori_loop(0, o + 1 - p, drain_side, 0)

    def drain_parts(t, carry):
        for r in range(pairs):
            to_mate(r, t).wait_send()
        for r in range(pairs - 1):
            to_far(r, t).wait_send()
        return carry

    lax.fori_loop(0, ntile, drain_parts, 0)


def body(nctx, nhead, hidden_in, w_query, w_key, w_value, w_output, vertical, slash_offsets):
    rows, feat = hidden_in.shape
    hd = w_key.shape[1]
    qw = w_query.shape[1]
    width = w_output.shape[1]
    wide = qw + 2 * hd
    nchunk = rows // PIECE
    pairs = nhead // 2
    outer = nctx // 2
    out_rows = rows // nhead
    assert out_rows == BS and nhead % 2 == 0 and nctx % 2 == 0
    tn = 512 if width % 512 == 0 else 128
    ntile = width // tn
    vmem = pl.BlockSpec(memory_space=pltpu.VMEM)
    smem = pl.BlockSpec(memory_space=pltpu.SMEM)
    hbm = pl.BlockSpec(memory_space=pl.ANY)
    dma = pltpu.SemaphoreType.DMA
    return pl.pallas_call(
        functools.partial(kernel, nctx, nhead),
        out_shape=pltpu.VMEM((out_rows, width), BF16),
        in_specs=[smem, smem, hbm, hbm, hbm, hbm, hbm],
        out_specs=vmem,
        scratch_shapes=[
            pltpu.VMEM((nhead, feat, wide), BF16),
            pltpu.VMEM((qw, width), BF16),
            pltpu.VMEM((rows, feat), BF16),
            pltpu.VMEM((pairs - 1, nchunk, PIECE, feat), BF16),
            pltpu.VMEM((pairs - 1, nchunk, PIECE, feat), BF16),
            pltpu.VMEM((rows, wide), F32),
            pltpu.VMEM((rows, qw), BF16),
            pltpu.VMEM((nctx * nchunk, PIECE, 2 * hd), BF16),
            pltpu.VMEM((pairs, ntile, BS, tn), BF16),
            pltpu.VMEM((pairs - 1, ntile, BS, tn), BF16),
            pltpu.VMEM((pairs, ntile, BS, tn), BF16),
            pltpu.VMEM((pairs - 1, ntile, BS, tn), BF16),
            pltpu.VMEM((2, BS, qw), BF16),
            pltpu.VMEM((rows, hd), F32),
            pltpu.VMEM((rows, hd), F32),
            pltpu.VMEM((rows, feat), BF16),
            dma((5,)),
            dma((1,)), dma((1,)),
            dma((pairs - 1, nchunk)), dma((pairs - 1, nchunk)),
            dma((pairs - 1, nchunk)), dma((pairs - 1, nchunk)),
            dma((nchunk, outer)), dma((nchunk, outer)),
            dma((nchunk, outer)), dma((nchunk, outer)),
            dma((pairs, ntile)), dma((pairs, ntile)),
            dma((pairs - 1, ntile)), dma((pairs - 1, ntile)),
        ],
        compiler_params=pltpu.CompilerParams(
            collective_id=0, has_side_effects=True, vmem_limit_bytes=62 * 1024 * 1024
        ),
        name="layer",
    )(
        vertical[0], slash_offsets[0], hidden_in,
        w_query.reshape(nhead, feat, qw), w_key.reshape(nhead, feat, hd),
        w_value.reshape(nhead, feat, hd), w_output,
    )


def solution(mesh):
    placed = (
        P("ctx", "head"),
        P(None, "head"),
        P(None, "head"),
        P(None, "head"),
        P("head", None),
        P("head", None, None),
        P("head", None, None),
    )
    return jax.shard_map(
        functools.partial(body, mesh.shape["ctx"], mesh.shape["head"]),
        mesh=mesh, in_specs=placed, out_specs=P(("ctx", "head"), None), check_vma=False,
    )
```

```python
import functools
import math

import jax
import jax.numpy as jnp
from jax import lax
from jax.experimental import pallas as pl
from jax.experimental.pallas import tpu as pltpu
from jax.sharding import PartitionSpec as P

BS = 128
PIECE = 16
TAIL = 4
STEP = 4
AHEAD = 1
THETA = 10000000.0
MESH = pl.DeviceIdType.MESH
F32 = jnp.float32
BF16 = jnp.bfloat16


def rope_rates(head_dim):
    lane = lax.broadcasted_iota(jnp.int32, (1, head_dim), 1)
    j = jnp.where(lane < head_dim // 2, lane, lane - head_dim // 2).astype(F32)
    return jnp.exp(-(j * 2.0 / head_dim) * math.log(THETA))


def kernel(
    nctx, nhead,
    vert, slash, hid, wq, wk, wv, wo,
    out,
    w_s, wo_s, mate_x, far_x, fwd_x, acc, q_s, kv, part_m, part_x, in_m, in_x, ctx_s, cos, sin, hid_s,
    wsem, ms, mr, fs, fr, gs, gr, cs, us, cr, ys, yr, above, near, pms, pmr, pxs, pxr,
):
    i, h = lax.axis_index("ctx"), lax.axis_index("head")
    o, p = i // 2, i % 2
    outer = nctx // 2
    pair, c0 = h // 2, h % 2
    pairs = nhead // 2
    hmate = h + 1 - 2 * c0
    ymate = i + 1 - 2 * p
    has_next, has_prev = o < outer - 1, o > 0
    nchunk, _, feat = hid.shape
    rows = nchunk * PIECE
    turns = nchunk // STEP
    final = turns - 1
    relayed = final
    per = BS // PIECE
    hd = cos.shape[1]
    qh = q_s.shape[1] // hd
    ntile, tn = part_m.shape[1], part_m.shape[3]

    def far(d):
        return lax.rem(pair + d, pairs) * 2 + c0

    qw = wq.shape[2]
    loads = [
        pltpu.make_async_copy(wq, w_s.at[:, :, pl.ds(0, qw)], wsem.at[0]),
        pltpu.make_async_copy(wk, w_s.at[:, :, pl.ds(qw, hd)], wsem.at[1]),
        pltpu.make_async_copy(wv, w_s.at[:, :, pl.ds(qw + hd, hd)], wsem.at[2]),
        pltpu.make_async_copy(wo, wo_s, wsem.at[3]),
    ]
    own = pltpu.make_async_copy(hid, hid_s, wsem.at[4])
    own.start()
    for load in loads:
        load.start()

    barrier = pltpu.get_barrier_semaphore()

    def greet(where):
        pl.semaphore_signal(barrier, inc=1, device_id=where, device_id_type=MESH)

    greet({"head": hmate})
    for d in range(1, pairs):
        greet({"head": far(d)})
    greet({"ctx": ymate})
    has_next, has_prev = o < outer - 1, o > 0

    @pl.when(has_next)
    def _():
        greet({"ctx": i + 2})

    @pl.when(has_prev)
    def _():
        greet({"ctx": i - 2})

    pl.semaphore_wait(
        barrier, pairs + 1 + jnp.where(has_next, 1, 0) + jnp.where(has_prev, 1, 0)
    )

    @pl.when(has_next & has_prev)
    def _():
        pl.semaphore_signal(near, inc=1, device_id={"ctx": i - 2}, device_id_type=MESH)

    def column_in():
        @pl.when(has_next)
        def _():
            pl.semaphore_wait(above, 1)

        @pl.when(has_prev)
        def _():
            pl.semaphore_signal(above, inc=1, device_id={"ctx": i - 2}, device_id_type=MESH)


    def remote(src, dst, send, recv, where):
        return pltpu.make_async_remote_copy(
            src_ref=src, dst_ref=dst, send_sem=send, recv_sem=recv,
            device_id=where, device_id_type=MESH,
        )

    def unit(t):
        if t == 0:
            return 0, 2 * STEP - TAIL
        return t * STEP + STEP - TAIL, TAIL if t == final else STEP

    def far_copy(d, t):
        u, n = unit(t)
        return remote(
            hid.at[pl.ds(u, n)], far_x.at[d - 1, pl.ds(u, n)],
            fs.at[d - 1, t], fr.at[d - 1, t], {"head": far(d)},
        )

    def fwd_copy(d, t):
        u, n = unit(t)
        return remote(
            far_x.at[d - 1, pl.ds(u, n)], fwd_x.at[d - 1, pl.ds(u, n)],
            gs.at[d - 1, t], gr.at[d - 1, t], {"head": hmate},
        )

    mate_copy = remote(hid, mate_x, ms.at[0], mr.at[0], {"head": hmate})
    for t in range(turns):
        for d in range(1, pairs):
            far_copy(d, t).start()
    mate_copy.start()

    def held_at(so, col, t):
        u, n = unit(t)
        return kv.at[pl.ds((so * 2 + col) * nchunk + u, n)]

    def each(low, high, act):
        if outer <= 4:
            for e in range(outer):
                @pl.when((e >= low) & (e < high))
                def _():
                    act(e)
        else:
            def one(e, carry):
                act(e)
                return carry

            lax.fori_loop(low, high, one, 0)

    def skip_copy(t, so, e):
        block = held_at(so, p, t)
        return remote(block, block, cs.at[t, e - 1, so], cr.at[t, so], {"ctx": i + 2 * e})

    def column_copy(t, so, e):
        block = held_at(so, p, t)
        return remote(block, block, us.at[e], cr.at[t, so], {"ctx": i + 2 * e})

    def skip(t, so):
        @pl.when(o < outer - 2)
        def _():
            skip_copy(t, so, 2).start()

        @pl.when(has_next)
        def _():
            skip_copy(t, so, 1).start()

    def side_copy(t, so, col):
        block = held_at(so, col, t)
        return remote(block, block, ys.at[t, so], yr.at[t, so], {"ctx": ymate})

    def relay(t, s):
        skip_copy(t, o - s, 1).wait_recv()
        if s % 2 == 0:
            skip(t, o - s)
        side_copy(t, o - s, p).start()

    def relays(t, low=0):
        for s in range(1, outer):
            c = t - (s + 1) // 2
            if low <= c < relayed:
                @pl.when(s <= o)
                def _():
                    relay(c, s)

    def cross(t, e):
        column_copy(t, o - e, e).wait_recv()
        side_copy(t, o - e, p).start()

    rates = rope_rates(hd)
    span = STEP * PIECE

    def table(c, carry):
        part = pl.ds(pl.multiple_of(c * span, span), span)
        spot = lax.broadcasted_iota(jnp.int32, (span, hd), 0) + (i * rows + c * span)
        angle = spot.astype(F32) * rates
        lane = lax.broadcasted_iota(jnp.int32, (span, hd), 1)
        sine = jnp.sin(angle)
        cos[part, :] = jnp.cos(angle)
        sin[part, :] = jnp.where(lane < hd // 2, -sine, sine)
        return carry

    lax.fori_loop(0, turns, table, 0)
    own.wait()
    for load in loads[:3]:
        load.wait()
    wide = w_s.shape[2]
    step = 256 if wide % 256 == 0 else 128

    def own_cols(t, carry):
        cols = pl.ds(pl.multiple_of(t * step, step), step)
        acc[:, cols] = jnp.dot(hid_s[...].reshape(rows, feat), w_s[h, :, cols], preferred_element_type=F32)
        return carry

    lax.fori_loop(0, wide // step, own_cols, 0)
    mate_copy.wait_recv()

    def mate_cols(t, carry):
        cols = pl.ds(pl.multiple_of(t * step, step), step)
        acc[:, cols] += jnp.dot(mate_x[...].reshape(rows, feat), w_s[hmate, :, cols], preferred_element_type=F32)
        return carry

    lax.fori_loop(0, wide // step, mate_cols, 0)

    kv_cols, q_cols = pl.ds(qw, 2 * hd), pl.ds(0, qw)
    def source(d):
        return lax.rem(pair + pairs - d, pairs) * 2

    def rope(x, part):
        return (x * cos[part, :] + pltpu.roll(x, hd // 2, 1) * sin[part, :]).astype(BF16)

    def project(t):
        u, n = unit(t)
        span = n * PIECE
        part = pl.ds(u * PIECE, span)
        both = acc[part, kv_cols]
        for d in range(1, pairs):
            far_copy(d, t).wait_recv()
            fwd_copy(d, t).start()
            both += jnp.dot(
                far_x[d - 1, pl.ds(u, n)].reshape(span, feat),
                w_s[source(d) + c0, :, kv_cols], preferred_element_type=F32,
            )
            fwd_copy(d, t).wait_recv()
            both += jnp.dot(
                fwd_x[d - 1, pl.ds(u, n)].reshape(span, feat),
                w_s[source(d) + 1 - c0, :, kv_cols], preferred_element_type=F32,
            )
        mine = pl.ds(i * nchunk + u, n)
        kv[mine, :, pl.ds(0, hd)] = rope(both[:, :hd], part).reshape(n, PIECE, hd)
        kv[mine, :, pl.ds(hd, hd)] = both[:, hd:].astype(BF16).reshape(n, PIECE, hd)

    def queries(t):
        u, n = unit(t)
        span = n * PIECE
        part = pl.ds(u * PIECE, span)
        mine = acc[part, q_cols]
        for d in range(1, pairs):
            mine += jnp.dot(
                far_x[d - 1, pl.ds(u, n)].reshape(span, feat), w_s[source(d) + c0, :, q_cols],
                preferred_element_type=F32,
            )
            mine += jnp.dot(
                fwd_x[d - 1, pl.ds(u, n)].reshape(span, feat),
                w_s[source(d) + 1 - c0, :, q_cols], preferred_element_type=F32,
            )
        for g in range(qh):
            q_s[part, pl.ds(g * hd, hd)] = rope(mine[:, g * hd:(g + 1) * hd], part)

    def emit(t):
        if t < relayed:
            skip(t, o)
        else:
            each(1, outer - o, lambda e: column_copy(t, o, outer - o - e).start())

        @pl.when(p == 0)
        def _():
            side_copy(t, o, p).start()

    for t in range(turns):
        if t == 0:
            @pl.when(o < outer - 2)
            def _():
                pl.semaphore_wait(near, 1)
        if t < final:
            @pl.when((t == outer - 1 - o) | ((t == final - 1) & (outer - 1 - o > t)))
            def _():
                column_in()

        project(t)
        emit(t)
        queries(t)
        relays(t)

    each(1, jnp.minimum(o + 1, 3), functools.partial(cross, final))
    relays(turns)
    each(3, o + 1, functools.partial(cross, final))
    for t in range(turns + 1, relayed + outer // 2):
        relays(t)

    for t in range(turns):
        each(0, o + p, lambda so: side_copy(t, so, 1 - p).wait_recv())
    loads[3].wait()

    nv, ns = vert.shape[1], slash.shape[1]
    scale = 1.0 / math.sqrt(hd)
    below = lax.broadcasted_iota(jnp.int32, (BS, BS), 1) <= lax.broadcasted_iota(
        jnp.int32, (BS, BS), 0
    )
    low = F32(-1e30)

    def attend(b, into):
        qb = i * (rows // BS) + b
        query_rows = pl.ds(pl.multiple_of(b * BS, BS), BS)

        def held(at, lanes):
            return kv[pl.ds(at * per, per), :, lanes].reshape(BS, hd)

        for g in range(qh):
            slots = [qb]
            live = [None]
            for s in range(ns + nv):
                slot = qb - slash[g, s] if s < ns else vert[g, s - ns]
                ok = (slot >= 0) & (slot < qb)
                for earlier in slots[1:]:
                    ok = ok & (slot != earlier)
                slots.append(slot)
                live.append(ok)
            query = q_s[query_rows, pl.ds(g * hd, hd)]
            at = [s if ok is None else jnp.where(ok, s, qb) for s, ok in zip(slots, live)]
            groups = [[0]] + [[n, n + 1] for n in range(1, len(at) - 1, 2)]
            if len(at) % 2 == 0:
                groups.append([len(at) - 1])
            scores = []
            for group in groups:
                keys = jnp.concatenate([held(at[n], pl.ds(0, hd)) for n in group], axis=0)
                both = lax.dot_general(
                    query, keys, (((1,), (1,)), ((), ())), preferred_element_type=F32
                ) * F32(scale)
                for m, n in enumerate(group):
                    sc = both[:, m * BS:(m + 1) * BS]
                    scores.append(jnp.where(below if n == 0 else live[n], sc, low))
            top = functools.reduce(jnp.maximum, scores)
            top = jnp.max(top, axis=1, keepdims=True)
            total = None
            summed = None
            for group in groups:
                raws = [jnp.exp(scores[n] - top) for n in group]
                for raw in raws:
                    total = raw if total is None else total + raw
                vals = jnp.concatenate([held(at[n], pl.ds(hd, hd)) for n in group], axis=0)
                weights = jnp.concatenate([raw.astype(BF16) for raw in raws], axis=1)
                add = jnp.dot(weights, vals, preferred_element_type=F32)
                summed = add if summed is None else summed + add
            total = jnp.sum(total, axis=1, keepdims=True)
            ctx_s[into, :, pl.ds(g * hd, hd)] = (summed / total).astype(BF16)

    def share(t, of):
        cols = pl.ds(pl.multiple_of(t * tn, tn), tn)
        return jnp.dot(ctx_s[of], wo_s[:, cols], preferred_element_type=F32)

    def to_mate(r, t):
        return remote(
            part_m.at[r, t], in_m.at[r, t], pms.at[r, t], pmr.at[r, t], {"head": hmate}
        )

    def to_far(r, t):
        return remote(
            part_x.at[r, t], in_x.at[r, t], pxs.at[r, t], pxr.at[r, t], {"head": far(r + 1)}
        )

    def give(r, t):
        part_m[r, t] = share(t, 0).astype(BF16)
        to_mate(r, t).start()

    def round_of(r, carry):
        to = lax.rem(pair + r + 1, pairs) * 2
        attend(to + 1 - c0, 0)
        for t in range(AHEAD):
            give(r, t)
        attend(to + c0, 1)

        def tile(t, carry):
            mine = share(t, 1)
            to_mate(r, t).wait_recv()
            part_x[r, t] = (mine + in_m[r, t].astype(F32)).astype(BF16)
            to_far(r, t).start()

            @pl.when(t + AHEAD < ntile)
            def _():
                give(r, t + AHEAD)

            return carry

        lax.fori_loop(0, ntile, tile, 0)
        return carry

    lax.fori_loop(0, pairs - 1, round_of, 0)
    attend(pair * 2 + 1 - c0, 0)

    def give_last(t, carry):
        give(pairs - 1, t)
        return carry

    lax.fori_loop(0, ntile, give_last, 0)
    attend(h, 1)

    def last(t, carry):
        mine = share(t, 1)
        to_mate(pairs - 1, t).wait_recv()
        mine = mine + in_m[pairs - 1, t].astype(F32)
        for r in range(pairs - 1):
            to_far(r, t).wait_recv()
            mine = mine + in_x[r, t].astype(F32)
        out[:, pl.ds(pl.multiple_of(t * tn, tn), tn)] = mine.astype(out.dtype)
        return carry

    lax.fori_loop(0, ntile, last, 0)

    mate_copy.wait_send()
    for t in range(turns):
        for d in range(1, pairs):
            far_copy(d, t).wait_send()
            fwd_copy(d, t).wait_send()
    def drain_skip(t):
        for s in range(0, outer, 2):
            @pl.when((s <= o) & (o < outer - 2))
            def _():
                skip_copy(t, o - s, 2).wait_send()

            @pl.when((s <= o) & has_next)
            def _():
                skip_copy(t, o - s, 1).wait_send()

    for t in range(relayed):
        drain_skip(t)

    for t in range(relayed, turns):
        each(1, outer - o, lambda e: column_copy(t, o, e).wait_send())

    for t in range(turns):
        each(0, o + 1 - p, lambda so: side_copy(t, so, p).wait_send())

    def drain_parts(t, carry):
        for r in range(pairs):
            to_mate(r, t).wait_send()
        for r in range(pairs - 1):
            to_far(r, t).wait_send()
        return carry

    lax.fori_loop(0, ntile, drain_parts, 0)


def body(nctx, nhead, hidden_in, w_query, w_key, w_value, w_output, vertical, slash_offsets):
    rows, feat = hidden_in.shape
    hd = w_key.shape[1]
    qw = w_query.shape[1]
    width = w_output.shape[1]
    wide = qw + 2 * hd
    nchunk = rows // PIECE
    turns = nchunk // STEP
    pairs = nhead // 2
    outer = nctx // 2
    out_rows = rows // nhead
    assert out_rows == BS and nhead % 2 == 0 and nctx % 2 == 0
    tn = 512 if width % 512 == 0 else 128
    ntile = width // tn
    vmem = pl.BlockSpec(memory_space=pltpu.VMEM)
    smem = pl.BlockSpec(memory_space=pltpu.SMEM)
    hbm = pl.BlockSpec(memory_space=pl.ANY)
    dma = pltpu.SemaphoreType.DMA
    return pl.pallas_call(
        functools.partial(kernel, nctx, nhead),
        out_shape=pltpu.VMEM((out_rows, width), BF16),
        in_specs=[smem, smem, hbm, hbm, hbm, hbm, hbm],
        out_specs=vmem,
        scratch_shapes=[
            pltpu.VMEM((nhead, feat, wide), BF16),
            pltpu.VMEM((qw, width), BF16),
            pltpu.VMEM((nchunk, PIECE, feat), BF16),
            pltpu.VMEM((pairs - 1, nchunk, PIECE, feat), BF16),
            pltpu.VMEM((pairs - 1, nchunk, PIECE, feat), BF16),
            pltpu.VMEM((rows, wide), F32),
            pltpu.VMEM((rows, qw), BF16),
            pltpu.VMEM((nctx * nchunk, PIECE, 2 * hd), BF16),
            pltpu.VMEM((pairs, ntile, BS, tn), BF16),
            pltpu.VMEM((pairs - 1, ntile, BS, tn), BF16),
            pltpu.VMEM((pairs, ntile, BS, tn), BF16),
            pltpu.VMEM((pairs - 1, ntile, BS, tn), BF16),
            pltpu.VMEM((2, BS, qw), BF16),
            pltpu.VMEM((rows, hd), F32),
            pltpu.VMEM((rows, hd), F32),
            pltpu.VMEM((nchunk, PIECE, feat), BF16),
            dma((5,)),
            dma((1,)), dma((1,)),
            dma((pairs - 1, turns)), dma((pairs - 1, turns)),
            dma((pairs - 1, turns)), dma((pairs - 1, turns)),
            dma((turns, 2, outer)), dma((outer,)), dma((turns, outer)),
            dma((turns, outer)), dma((turns, outer)),
            pltpu.SemaphoreType.REGULAR, pltpu.SemaphoreType.REGULAR,
            dma((pairs, ntile)), dma((pairs, ntile)),
            dma((pairs - 1, ntile)), dma((pairs - 1, ntile)),
        ],
        compiler_params=pltpu.CompilerParams(
            collective_id=0, has_side_effects=True, vmem_limit_bytes=62 * 1024 * 1024
        ),
        name="layer",
    )(
        vertical[0], slash_offsets[0], hidden_in.reshape(nchunk, PIECE, feat),
        w_query.reshape(nhead, feat, qw), w_key.reshape(nhead, feat, hd),
        w_value.reshape(nhead, feat, hd), w_output,
    )


def solution(mesh):
    placed = (
        P("ctx", "head"),
        P(None, "head"),
        P(None, "head"),
        P(None, "head"),
        P("head", None),
        P("head", None, None),
        P("head", None, None),
    )
    return jax.shard_map(
        functools.partial(body, mesh.shape["ctx"], mesh.shape["head"]),
        mesh=mesh, in_specs=placed, out_specs=P(("ctx", "head"), None), check_vma=False,
    )
```

```python
import functools
import math

import jax
import jax.numpy as jnp
from jax import lax
from jax.experimental import pallas as pl
from jax.experimental.pallas import tpu as pltpu
from jax.sharding import PartitionSpec as P

BS = 128
PIECE = 64
AHEAD = 1
LENT = (1, 0)
PASS_AT = 5
THETA = 10000000.0
MESH = pl.DeviceIdType.MESH
F32 = jnp.float32
BF16 = jnp.bfloat16


def rope_rates(head_dim):
    lane = lax.broadcasted_iota(jnp.int32, (1, head_dim), 1)
    j = jnp.where(lane < head_dim // 2, lane, lane - head_dim // 2).astype(F32)
    return jnp.exp(-(j * 2.0 / head_dim) * math.log(THETA))


def kernel(
    nctx, nhead,
    vert, slash, hid, wq, wk, wv, wo,
    out,
    w_s, wo_s, mate_x, far_x, fwd_x, acc, q_s, kv, part_m, part_x, in_m, in_x, ctx_s, cos, sin, hid_s,
    wsem, ms, mr, fs, fr, gs, gr, cs, cr, ys, yr, pms, pmr, pxs, pxr, lent_x, ls, lr, os,
):
    i, h = lax.axis_index("ctx"), lax.axis_index("head")
    o, p = i // 2, i % 2
    outer = nctx // 2
    pair, c0 = h // 2, h % 2
    pairs = nhead // 2
    hmate = h + 1 - 2 * c0
    ymate = i + 1 - 2 * p
    has_next, has_prev = o < outer - 1, o > 0
    rows = hid.shape[0]
    nchunk = rows // PIECE
    per = BS // PIECE
    hd = cos.shape[1]
    qh = q_s.shape[1] // hd
    ntile, tn = part_m.shape[1], part_m.shape[3]

    def far(d):
        return lax.rem(pair + d, pairs) * 2 + c0

    qw = wq.shape[2]
    loads = [
        pltpu.make_async_copy(wq, w_s.at[:, :, pl.ds(0, qw)], wsem.at[0]),
        pltpu.make_async_copy(wk, w_s.at[:, :, pl.ds(qw, hd)], wsem.at[1]),
        pltpu.make_async_copy(wv, w_s.at[:, :, pl.ds(qw + hd, hd)], wsem.at[2]),
        pltpu.make_async_copy(wo, wo_s, wsem.at[3]),
    ]
    own = pltpu.make_async_copy(hid, hid_s, wsem.at[4])
    own.start()
    for load in loads:
        load.start()

    barrier = pltpu.get_barrier_semaphore()

    def greet(where):
        pl.semaphore_signal(barrier, inc=1, device_id=where, device_id_type=MESH)

    greet({"head": hmate})
    for d in range(1, pairs):
        greet({"head": far(d)})
    greet({"ctx": ymate})

    @pl.when(has_next)
    def _():
        greet({"ctx": i + 2})

    @pl.when(has_prev)
    def _():
        greet({"ctx": i - 2})

    pl.semaphore_wait(
        barrier, pairs + 1 + jnp.where(has_next, 1, 0) + jnp.where(has_prev, 1, 0)
    )

    def remote(src, dst, send, recv, where):
        return pltpu.make_async_remote_copy(
            src_ref=src, dst_ref=dst, send_sem=send, recv_sem=recv,
            device_id=where, device_id_type=MESH,
        )

    def far_copy(d, c):
        return remote(
            hid.at[pl.ds(c * PIECE, PIECE), :], far_x.at[d - 1, c],
            fs.at[d - 1, c], fr.at[d - 1, c], {"head": far(d)},
        )

    def fwd_copy(d, c):
        return remote(
            far_x.at[d - 1, c], fwd_x.at[d - 1, c],
            gs.at[d - 1, c], gr.at[d - 1, c], {"head": hmate},
        )

    mate_copy = remote(hid, mate_x, ms.at[0], mr.at[0], {"head": hmate})
    for c in range(nchunk):
        for d in range(1, pairs):
            far_copy(d, c).start()
    mate_copy.start()

    def next_copy(c, so):
        block = kv.at[(so * 2 + p) * nchunk + c]
        return remote(block, block, cs.at[c, so], cr.at[c, so], {"ctx": i + 2})

    def side_copy(c, so, col):
        block = kv.at[(so * 2 + col) * nchunk + c]
        return remote(block, block, ys.at[c, so], yr.at[c, so], {"ctx": ymate})

    def relay(c, so):
        next_copy(c, so).wait_recv()

        @pl.when(has_next)
        def _():
            next_copy(c, so).start()

        side_copy(c, so, p).start()

    rates = rope_rates(hd)

    def table(c, carry):
        part = pl.ds(pl.multiple_of(c * PIECE, PIECE), PIECE)
        spot = lax.broadcasted_iota(jnp.int32, (PIECE, hd), 0) + (i * rows + c * PIECE)
        angle = spot.astype(F32) * rates
        lane = lax.broadcasted_iota(jnp.int32, (PIECE, hd), 1)
        sine = jnp.sin(angle)
        cos[part, :] = jnp.cos(angle)
        sin[part, :] = jnp.where(lane < hd // 2, -sine, sine)
        return carry

    lax.fori_loop(0, nchunk, table, 0)
    own.wait()
    for load in loads[:3]:
        load.wait()
    wide = w_s.shape[2]
    step = 256 if wide % 256 == 0 else 128

    def own_cols(t, carry):
        cols = pl.ds(pl.multiple_of(t * step, step), step)
        acc[:, cols] = jnp.dot(hid_s[...], w_s[h, :, cols], preferred_element_type=F32)
        return carry

    lax.fori_loop(0, wide // step, own_cols, 0)
    mate_copy.wait_recv()

    def mate_cols(t, carry):
        cols = pl.ds(pl.multiple_of(t * step, step), step)
        acc[:, cols] += jnp.dot(mate_x[...], w_s[hmate, :, cols], preferred_element_type=F32)
        return carry

    lax.fori_loop(0, wide // step, mate_cols, 0)

    def project(c):
        part = pl.ds(pl.multiple_of(c * PIECE, PIECE), PIECE)
        for d in range(1, pairs):
            far_copy(d, c).wait_recv()
            fwd_copy(d, c).start()
            src = lax.rem(pair + pairs - d, pairs) * 2
            acc[part, :] += jnp.dot(
                far_x[d - 1, c], w_s[src + c0], preferred_element_type=F32
            )
            fwd_copy(d, c).wait_recv()
            acc[part, :] += jnp.dot(
                fwd_x[d - 1, c], w_s[src + 1 - c0], preferred_element_type=F32
            )
        cosine, sine = cos[part, :], sin[part, :]

        def rope(u):
            return (u * cosine + pltpu.roll(u, hd // 2, 1) * sine).astype(BF16)

        mine = i * nchunk + c
        kv[mine, :, pl.ds(0, hd)] = rope(acc[part, pl.ds(qw, hd)])
        kv[mine, :, pl.ds(hd, hd)] = acc[part, pl.ds(qw + hd, hd)].astype(BF16)

        @pl.when(has_next)
        def _():
            next_copy(c, o).start()

        @pl.when(p == 0)
        def _():
            side_copy(c, o, p).start()

        for g in range(qh):
            q_s[part, pl.ds(g * hd, hd)] = rope(acc[part, pl.ds(g * hd, hd)])

    def turn(t, carry):
        @pl.when(t < nchunk)
        def _():
            project(t)

        for c in range(nchunk):
            s = t - c

            @pl.when((s >= 1) & (s <= o))
            def _():
                relay(c, o - s)

        return carry

    lax.fori_loop(0, nchunk + outer - 1, turn, 0)

    def passed(so, carry):
        for c in range(nchunk):
            side_copy(c, so, 1 - p).wait_recv()
        return carry

    lax.fori_loop(0, o + p, passed, 0)
    loads[3].wait()

    nv, ns = vert.shape[1], slash.shape[1]
    scale = 1.0 / math.sqrt(hd)
    below = lax.broadcasted_iota(jnp.int32, (BS, BS), 1) <= lax.broadcasted_iota(
        jnp.int32, (BS, BS), 0
    )
    low = F32(-1e30)

    def attend(b, into):
        qb = i * (rows // BS) + b
        query_rows = pl.ds(pl.multiple_of(b * BS, BS), BS)

        def held(at, lanes):
            return kv[pl.ds(at * per, per), :, lanes].reshape(BS, hd)

        for g in range(qh):
            slots = [qb]
            live = [None]
            for s in range(ns + nv):
                slot = qb - slash[g, s] if s < ns else vert[g, s - ns]
                ok = (slot >= 0) & (slot < qb)
                for earlier in slots[1:]:
                    ok = ok & (slot != earlier)
                slots.append(slot)
                live.append(ok)
            query = q_s[query_rows, pl.ds(g * hd, hd)]
            at = [s if ok is None else jnp.where(ok, s, qb) for s, ok in zip(slots, live)]
            groups = [[0]] + [[n, n + 1] for n in range(1, len(at) - 1, 2)]
            if len(at) % 2 == 0:
                groups.append([len(at) - 1])
            scores = []
            for group in groups:
                keys = jnp.concatenate([held(at[n], pl.ds(0, hd)) for n in group], axis=0)
                both = lax.dot_general(
                    query, keys, (((1,), (1,)), ((), ())), preferred_element_type=F32
                ) * F32(scale)
                for m, n in enumerate(group):
                    sc = both[:, m * BS:(m + 1) * BS]
                    scores.append(jnp.where(below if n == 0 else live[n], sc, low))
            top = functools.reduce(jnp.maximum, scores)
            top = jnp.max(top, axis=1, keepdims=True)
            total = None
            summed = None
            for group in groups:
                raws = [jnp.exp(scores[n] - top) for n in group]
                for raw in raws:
                    total = raw if total is None else total + raw
                vals = jnp.concatenate([held(at[n], pl.ds(hd, hd)) for n in group], axis=0)
                weights = jnp.concatenate([raw.astype(BF16) for raw in raws], axis=1)
                add = jnp.dot(weights, vals, preferred_element_type=F32)
                summed = add if summed is None else summed + add
            total = jnp.sum(total, axis=1, keepdims=True)
            ctx_s[into, :, pl.ds(g * hd, hd)] = (summed / total).astype(BF16)

    def share(t, of):
        cols = pl.ds(pl.multiple_of(t * tn, tn), tn)
        return jnp.dot(ctx_s[of], wo_s[:, cols], preferred_element_type=F32)

    def to_mate(r, t):
        return remote(
            part_m.at[r, t], in_m.at[r, t], pms.at[r, t], pmr.at[r, t], {"head": hmate}
        )

    def to_far(r, t):
        return remote(
            part_x.at[r, t], in_x.at[r, t], pxs.at[r, t], pxr.at[r, t], {"head": far(r + 1)}
        )

    helpers = outer // 4
    kind = lax.rem(outer - 1 - o, 2)
    helper = (outer - 1 - o) // 2
    lends = helper < helpers
    base = kind * LENT[0]
    count = jnp.where(lends, jnp.where(kind == 0, LENT[0], LENT[1]), 0)

    def is_lent(r, t):
        return (r == 0) & (t >= 1) & (t < 1 + count)

    def lend(t):
        return remote(
            part_x.at[0, t], lent_x.at[base + t - 1], ls.at[t - 1], lr.at[base + t - 1],
            {"ctx": helper * 2 + p, "head": far(1)},
        )

    def pass_on(slot):
        late, first = (0, 0) if slot < LENT[0] else (1, LENT[0])
        t = 1 + slot - first
        return remote(
            lent_x.at[slot], in_x.at[0, t], os.at[slot], pxr.at[0, t],
            {"ctx": (outer - 1 - 2 * o - late) * 2 + p},
        )

    def landed(slot):
        return remote(
            lent_x.at[slot], lent_x.at[slot], os.at[slot], lr.at[slot], {"head": far(1)},
        )

    def give(r, t):
        part_m[r, t] = share(t, 0).astype(BF16)
        to_mate(r, t).start()

    def round_of(r, carry):
        to = lax.rem(pair + r + 1, pairs) * 2
        attend(to + 1 - c0, 0)
        for t in range(AHEAD):
            give(r, t)
        attend(to + c0, 1)

        def tile(t, carry):
            mine = share(t, 1)
            to_mate(r, t).wait_recv()
            part_x[r, t] = (mine + in_m[r, t].astype(F32)).astype(BF16)
            away = is_lent(r, t)

            @pl.when(away)
            def _():
                lend(t).start()

            @pl.when(jnp.logical_not(away))
            def _():
                to_far(r, t).start()

            @pl.when(t + AHEAD < ntile)
            def _():
                give(r, t + AHEAD)

            return carry

        lax.fori_loop(0, ntile, tile, 0)
        return carry

    lax.fori_loop(0, pairs - 1, round_of, 0)
    attend(pair * 2 + 1 - c0, 0)

    def give_last(t, carry):
        give(pairs - 1, t)
        return carry

    lax.fori_loop(0, ntile, give_last, 0)
    attend(h, 1)

    def last(t, carry):
        if helpers:
            @pl.when((t == min(PASS_AT, ntile - 1)) & (o < helpers))
            def _():
                for slot in range(sum(LENT)):
                    landed(slot).wait_recv()
                    pass_on(slot).start()

        mine = share(t, 1)
        to_mate(pairs - 1, t).wait_recv()
        mine = mine + in_m[pairs - 1, t].astype(F32)
        for r in range(pairs - 1):
            to_far(r, t).wait_recv()
            mine = mine + in_x[r, t].astype(F32)
        out[:, pl.ds(pl.multiple_of(t * tn, tn), tn)] = mine.astype(out.dtype)
        return carry

    lax.fori_loop(0, ntile, last, 0)

    mate_copy.wait_send()
    for c in range(nchunk):
        for d in range(1, pairs):
            far_copy(d, c).wait_send()
            fwd_copy(d, c).wait_send()

    def drain_next(so, carry):
        for c in range(nchunk):
            next_copy(c, so).wait_send()
        return carry

    lax.fori_loop(0, jnp.where(has_next, o + 1, 0), drain_next, 0)

    def drain_side(so, carry):
        for c in range(nchunk):
            side_copy(c, so, p).wait_send()
        return carry

    lax.fori_loop(0, o + 1 - p, drain_side, 0)

    def drain_parts(t, carry):
        for r in range(pairs):
            to_mate(r, t).wait_send()
        for r in range(pairs - 1):
            away = is_lent(r, t)

            @pl.when(away)
            def _():
                lend(t).wait_send()

            @pl.when(jnp.logical_not(away))
            def _():
                to_far(r, t).wait_send()
        return carry

    lax.fori_loop(0, ntile, drain_parts, 0)

    if helpers:
        @pl.when(o < helpers)
        def _():
            for slot in range(sum(LENT)):
                pass_on(slot).wait_send()


def body(nctx, nhead, hidden_in, w_query, w_key, w_value, w_output, vertical, slash_offsets):
    rows, feat = hidden_in.shape
    hd = w_key.shape[1]
    qw = w_query.shape[1]
    width = w_output.shape[1]
    wide = qw + 2 * hd
    nchunk = rows // PIECE
    pairs = nhead // 2
    outer = nctx // 2
    out_rows = rows // nhead
    assert out_rows == BS and nhead % 2 == 0 and nctx % 2 == 0
    tn = 512 if width % 512 == 0 else 128
    ntile = width // tn
    vmem = pl.BlockSpec(memory_space=pltpu.VMEM)
    smem = pl.BlockSpec(memory_space=pltpu.SMEM)
    hbm = pl.BlockSpec(memory_space=pl.ANY)
    dma = pltpu.SemaphoreType.DMA
    return pl.pallas_call(
        functools.partial(kernel, nctx, nhead),
        out_shape=pltpu.VMEM((out_rows, width), BF16),
        in_specs=[smem, smem, hbm, hbm, hbm, hbm, hbm],
        out_specs=vmem,
        scratch_shapes=[
            pltpu.VMEM((nhead, feat, wide), BF16),
            pltpu.VMEM((qw, width), BF16),
            pltpu.VMEM((rows, feat), BF16),
            pltpu.VMEM((pairs - 1, nchunk, PIECE, feat), BF16),
            pltpu.VMEM((pairs - 1, nchunk, PIECE, feat), BF16),
            pltpu.VMEM((rows, wide), F32),
            pltpu.VMEM((rows, qw), BF16),
            pltpu.VMEM((nctx * nchunk, PIECE, 2 * hd), BF16),
            pltpu.VMEM((pairs, ntile, BS, tn), BF16),
            pltpu.VMEM((pairs - 1, ntile, BS, tn), BF16),
            pltpu.VMEM((pairs, ntile, BS, tn), BF16),
            pltpu.VMEM((pairs - 1, ntile, BS, tn), BF16),
            pltpu.VMEM((2, BS, qw), BF16),
            pltpu.VMEM((rows, hd), F32),
            pltpu.VMEM((rows, hd), F32),
            pltpu.VMEM((rows, feat), BF16),
            dma((5,)),
            dma((1,)), dma((1,)),
            dma((pairs - 1, nchunk)), dma((pairs - 1, nchunk)),
            dma((pairs - 1, nchunk)), dma((pairs - 1, nchunk)),
            dma((nchunk, outer)), dma((nchunk, outer)),
            dma((nchunk, outer)), dma((nchunk, outer)),
            dma((pairs, ntile)), dma((pairs, ntile)),
            dma((pairs - 1, ntile)), dma((pairs - 1, ntile)),
            pltpu.VMEM((sum(LENT), BS, tn), BF16),
            dma((max(LENT),)), dma((sum(LENT),)), dma((sum(LENT),)),
        ],
        compiler_params=pltpu.CompilerParams(
            collective_id=0, has_side_effects=True, vmem_limit_bytes=62 * 1024 * 1024
        ),
        name="layer",
    )(
        vertical[0], slash_offsets[0], hidden_in,
        w_query.reshape(nhead, feat, qw), w_key.reshape(nhead, feat, hd),
        w_value.reshape(nhead, feat, hd), w_output,
    )


def solution(mesh):
    placed = (
        P("ctx", "head"),
        P(None, "head"),
        P(None, "head"),
        P(None, "head"),
        P("head", None),
        P("head", None, None),
        P("head", None, None),
    )
    return jax.shard_map(
        functools.partial(body, mesh.shape["ctx"], mesh.shape["head"]),
        mesh=mesh, in_specs=placed, out_specs=P(("ctx", "head"), None), check_vma=False,
    )
```

```python
import functools
import math

import jax
import jax.numpy as jnp
from jax import lax
from jax.experimental import pallas as pl
from jax.experimental.pallas import tpu as pltpu
from jax.sharding import PartitionSpec as P

BS = 128
PIECE = 64
AHEAD = 1
LENT = (3, 1)
PASS_AT = 3
THETA = 10000000.0
MESH = pl.DeviceIdType.MESH
F32 = jnp.float32
BF16 = jnp.bfloat16


def rope_rates(head_dim):
    lane = lax.broadcasted_iota(jnp.int32, (1, head_dim), 1)
    j = jnp.where(lane < head_dim // 2, lane, lane - head_dim // 2).astype(F32)
    return jnp.exp(-(j * 2.0 / head_dim) * math.log(THETA))


def kernel(
    nctx, nhead,
    vert, slash, hid, wq, wk, wv, wo,
    out,
    w_s, wo_s, mate_x, far_x, fwd_x, acc, q_s, kv, part_m, part_x, in_m, in_x, ctx_s, cos, sin, hid_s,
    wsem, ms, mr, fs, fr, gs, gr, cs, cr, ys, yr, pms, pmr, pxs, pxr, lent_x, ls, lr, os,
):
    i, h = lax.axis_index("ctx"), lax.axis_index("head")
    o, p = i // 2, i % 2
    outer = nctx // 2
    pair, c0 = h // 2, h % 2
    pairs = nhead // 2
    hmate = h + 1 - 2 * c0
    ymate = i + 1 - 2 * p
    has_next, has_prev = o < outer - 1, o > 0
    rows = hid.shape[0]
    nchunk = rows // PIECE
    per = BS // PIECE
    hd = cos.shape[1]
    qh = q_s.shape[1] // hd
    ntile, tn = part_m.shape[1], part_m.shape[3]

    def far(d):
        return lax.rem(pair + d, pairs) * 2 + c0

    qw = wq.shape[2]
    loads = [
        pltpu.make_async_copy(wq, w_s.at[:, :, pl.ds(0, qw)], wsem.at[0]),
        pltpu.make_async_copy(wk, w_s.at[:, :, pl.ds(qw, hd)], wsem.at[1]),
        pltpu.make_async_copy(wv, w_s.at[:, :, pl.ds(qw + hd, hd)], wsem.at[2]),
        pltpu.make_async_copy(wo, wo_s, wsem.at[3]),
    ]
    own = pltpu.make_async_copy(hid, hid_s, wsem.at[4])
    own.start()
    for load in loads:
        load.start()

    barrier = pltpu.get_barrier_semaphore()

    def greet(where):
        pl.semaphore_signal(barrier, inc=1, device_id=where, device_id_type=MESH)

    greet({"head": hmate})
    for d in range(1, pairs):
        greet({"head": far(d)})
    greet({"ctx": ymate})

    @pl.when(has_next)
    def _():
        greet({"ctx": i + 2})

    @pl.when(has_prev)
    def _():
        greet({"ctx": i - 2})

    pl.semaphore_wait(
        barrier, pairs + 1 + jnp.where(has_next, 1, 0) + jnp.where(has_prev, 1, 0)
    )

    def remote(src, dst, send, recv, where):
        return pltpu.make_async_remote_copy(
            src_ref=src, dst_ref=dst, send_sem=send, recv_sem=recv,
            device_id=where, device_id_type=MESH,
        )

    def far_copy(d, c):
        return remote(
            hid.at[pl.ds(c * PIECE, PIECE), :], far_x.at[d - 1, c],
            fs.at[d - 1, c], fr.at[d - 1, c], {"head": far(d)},
        )

    def fwd_copy(d, c):
        return remote(
            far_x.at[d - 1, c], fwd_x.at[d - 1, c],
            gs.at[d - 1, c], gr.at[d - 1, c], {"head": hmate},
        )

    mate_copy = remote(hid, mate_x, ms.at[0], mr.at[0], {"head": hmate})
    for c in range(nchunk):
        for d in range(1, pairs):
            far_copy(d, c).start()
    mate_copy.start()

    def next_copy(c, so):
        block = kv.at[(so * 2 + p) * nchunk + c]
        return remote(block, block, cs.at[c, so], cr.at[c, so], {"ctx": i + 2})

    def side_copy(c, so, col):
        block = kv.at[(so * 2 + col) * nchunk + c]
        return remote(block, block, ys.at[c, so], yr.at[c, so], {"ctx": ymate})

    def relay(c, so):
        next_copy(c, so).wait_recv()

        @pl.when(has_next)
        def _():
            next_copy(c, so).start()

        side_copy(c, so, p).start()

    rates = rope_rates(hd)

    def table(c, carry):
        part = pl.ds(pl.multiple_of(c * PIECE, PIECE), PIECE)
        spot = lax.broadcasted_iota(jnp.int32, (PIECE, hd), 0) + (i * rows + c * PIECE)
        angle = spot.astype(F32) * rates
        lane = lax.broadcasted_iota(jnp.int32, (PIECE, hd), 1)
        sine = jnp.sin(angle)
        cos[part, :] = jnp.cos(angle)
        sin[part, :] = jnp.where(lane < hd // 2, -sine, sine)
        return carry

    lax.fori_loop(0, nchunk, table, 0)
    own.wait()
    for load in loads[:3]:
        load.wait()
    wide = w_s.shape[2]
    step = 256 if wide % 256 == 0 else 128

    def own_cols(t, carry):
        cols = pl.ds(pl.multiple_of(t * step, step), step)
        acc[:, cols] = jnp.dot(hid_s[...], w_s[h, :, cols], preferred_element_type=F32)
        return carry

    lax.fori_loop(0, wide // step, own_cols, 0)
    mate_copy.wait_recv()

    def mate_cols(t, carry):
        cols = pl.ds(pl.multiple_of(t * step, step), step)
        acc[:, cols] += jnp.dot(mate_x[...], w_s[hmate, :, cols], preferred_element_type=F32)
        return carry

    lax.fori_loop(0, wide // step, mate_cols, 0)

    def project(c):
        part = pl.ds(pl.multiple_of(c * PIECE, PIECE), PIECE)
        for d in range(1, pairs):
            far_copy(d, c).wait_recv()
            fwd_copy(d, c).start()
            src = lax.rem(pair + pairs - d, pairs) * 2
            acc[part, :] += jnp.dot(
                far_x[d - 1, c], w_s[src + c0], preferred_element_type=F32
            )
            fwd_copy(d, c).wait_recv()
            acc[part, :] += jnp.dot(
                fwd_x[d - 1, c], w_s[src + 1 - c0], preferred_element_type=F32
            )
        cosine, sine = cos[part, :], sin[part, :]

        def rope(u):
            return (u * cosine + pltpu.roll(u, hd // 2, 1) * sine).astype(BF16)

        mine = i * nchunk + c
        kv[mine, :, pl.ds(0, hd)] = rope(acc[part, pl.ds(qw, hd)])
        kv[mine, :, pl.ds(hd, hd)] = acc[part, pl.ds(qw + hd, hd)].astype(BF16)

        @pl.when(has_next)
        def _():
            next_copy(c, o).start()

        @pl.when(p == 0)
        def _():
            side_copy(c, o, p).start()

        for g in range(qh):
            q_s[part, pl.ds(g * hd, hd)] = rope(acc[part, pl.ds(g * hd, hd)])

    def turn(t, carry):
        @pl.when(t < nchunk)
        def _():
            project(t)

        for c in range(nchunk):
            s = t - c

            @pl.when((s >= 1) & (s <= o))
            def _():
                relay(c, o - s)

        return carry

    lax.fori_loop(0, nchunk + outer - 1, turn, 0)

    def passed(so, carry):
        for c in range(nchunk):
            side_copy(c, so, 1 - p).wait_recv()
        return carry

    lax.fori_loop(0, o + p, passed, 0)
    loads[3].wait()

    nv, ns = vert.shape[1], slash.shape[1]
    scale = 1.0 / math.sqrt(hd)
    below = lax.broadcasted_iota(jnp.int32, (BS, BS), 1) <= lax.broadcasted_iota(
        jnp.int32, (BS, BS), 0
    )
    low = F32(-1e30)

    def attend(b, into):
        qb = i * (rows // BS) + b
        query_rows = pl.ds(pl.multiple_of(b * BS, BS), BS)

        def held(at, lanes):
            return kv[pl.ds(at * per, per), :, lanes].reshape(BS, hd)

        for g in range(qh):
            slots = [qb]
            live = [None]
            for s in range(ns + nv):
                slot = qb - slash[g, s] if s < ns else vert[g, s - ns]
                ok = (slot >= 0) & (slot < qb)
                for earlier in slots[1:]:
                    ok = ok & (slot != earlier)
                slots.append(slot)
                live.append(ok)
            query = q_s[query_rows, pl.ds(g * hd, hd)]
            at = [s if ok is None else jnp.where(ok, s, qb) for s, ok in zip(slots, live)]
            groups = [[0]] + [[n, n + 1] for n in range(1, len(at) - 1, 2)]
            if len(at) % 2 == 0:
                groups.append([len(at) - 1])
            scores = []
            for group in groups:
                keys = jnp.concatenate([held(at[n], pl.ds(0, hd)) for n in group], axis=0)
                both = lax.dot_general(
                    query, keys, (((1,), (1,)), ((), ())), preferred_element_type=F32
                ) * F32(scale)
                for m, n in enumerate(group):
                    sc = both[:, m * BS:(m + 1) * BS]
                    scores.append(jnp.where(below if n == 0 else live[n], sc, low))
            top = functools.reduce(jnp.maximum, scores)
            top = jnp.max(top, axis=1, keepdims=True)
            total = None
            summed = None
            for group in groups:
                raws = [jnp.exp(scores[n] - top) for n in group]
                for raw in raws:
                    total = raw if total is None else total + raw
                vals = jnp.concatenate([held(at[n], pl.ds(hd, hd)) for n in group], axis=0)
                weights = jnp.concatenate([raw.astype(BF16) for raw in raws], axis=1)
                add = jnp.dot(weights, vals, preferred_element_type=F32)
                summed = add if summed is None else summed + add
            total = jnp.sum(total, axis=1, keepdims=True)
            ctx_s[into, :, pl.ds(g * hd, hd)] = (summed / total).astype(BF16)

    def share(t, of):
        cols = pl.ds(pl.multiple_of(t * tn, tn), tn)
        return jnp.dot(ctx_s[of], wo_s[:, cols], preferred_element_type=F32)

    def to_mate(r, t):
        return remote(
            part_m.at[r, t], in_m.at[r, t], pms.at[r, t], pmr.at[r, t], {"head": hmate}
        )

    helped = outer - 1 - o
    helps = o < outer // 2
    lends = o >= outer - outer // 2

    half = tn // 2

    def lent_by(q):
        return jnp.where(q >= outer - outer // 4, LENT[0], LENT[1])

    count = jnp.where(lends, lent_by(o), 0)
    taken = jnp.where(helps, lent_by(helped), 0)

    def to_far(r, u):
        return remote(
            part_x.at[r, u], in_x.at[r, u], pxs.at[r, u], pxr.at[r, u], {"head": far(r + 1)}
        )

    def is_lent(r, u):
        return (r == 0) & (u >= 2) & (u < 2 + count)

    def lend(u):
        return remote(
            part_x.at[0, u], lent_x.at[u - 2], ls.at[u - 2], lr.at[u - 2],
            {"ctx": helped * 2 + p, "head": far(1)},
        )

    def pass_on(slot):
        return remote(
            lent_x.at[slot], in_x.at[0, 2 + slot], os.at[slot], pxr.at[0, 2 + slot],
            {"ctx": helped * 2 + p},
        )

    def landed(slot):
        return remote(
            lent_x.at[slot], lent_x.at[slot], os.at[slot], lr.at[slot], {"head": far(1)},
        )

    def give(r, t):
        part_m[r, t] = share(t, 0).astype(BF16)
        to_mate(r, t).start()

    def round_of(r, carry):
        to = lax.rem(pair + r + 1, pairs) * 2
        attend(to + 1 - c0, 0)
        for t in range(AHEAD):
            give(r, t)
        attend(to + c0, 1)

        def tile(t, carry):
            mine = share(t, 1)
            to_mate(r, t).wait_recv()
            mine = (mine + in_m[r, t].astype(F32)).astype(BF16)
            for k in range(2):
                u = 2 * t + k
                part_x[r, u] = mine[:, k * half:(k + 1) * half]
                away = is_lent(r, u)

                @pl.when(away)
                def _():
                    lend(u).start()

                @pl.when(jnp.logical_not(away))
                def _():
                    to_far(r, u).start()

            @pl.when(t + AHEAD < ntile)
            def _():
                give(r, t + AHEAD)

            return carry

        lax.fori_loop(0, ntile, tile, 0)
        return carry

    lax.fori_loop(0, pairs - 1, round_of, 0)
    attend(pair * 2 + 1 - c0, 0)

    def give_last(t, carry):
        give(pairs - 1, t)
        return carry

    lax.fori_loop(0, ntile, give_last, 0)
    attend(h, 1)

    def last(t, carry):
        for slot in range(max(LENT)):
            @pl.when((t == min(PASS_AT, ntile - 1)) & (slot < taken))
            def _():
                landed(slot).wait_recv()
                pass_on(slot).start()

        mine = share(t, 1)
        to_mate(pairs - 1, t).wait_recv()
        mine = mine + in_m[pairs - 1, t].astype(F32)
        for k in range(2):
            u = 2 * t + k
            part = mine[:, k * half:(k + 1) * half]
            for r in range(pairs - 1):
                to_far(r, u).wait_recv()
                part = part + in_x[r, u].astype(F32)
            cols = pl.ds(pl.multiple_of(u * half, half), half)
            out[:, cols] = part.astype(out.dtype)
        return carry

    lax.fori_loop(0, ntile, last, 0)

    mate_copy.wait_send()
    for c in range(nchunk):
        for d in range(1, pairs):
            far_copy(d, c).wait_send()
            fwd_copy(d, c).wait_send()

    def drain_next(so, carry):
        for c in range(nchunk):
            next_copy(c, so).wait_send()
        return carry

    lax.fori_loop(0, jnp.where(has_next, o + 1, 0), drain_next, 0)

    def drain_side(so, carry):
        for c in range(nchunk):
            side_copy(c, so, p).wait_send()
        return carry

    lax.fori_loop(0, o + 1 - p, drain_side, 0)

    def drain_parts(t, carry):
        for r in range(pairs):
            to_mate(r, t).wait_send()
        for r in range(pairs - 1):
            for k in range(2):
                u = 2 * t + k
                away = is_lent(r, u)

                @pl.when(away)
                def _():
                    lend(u).wait_send()

                @pl.when(jnp.logical_not(away))
                def _():
                    to_far(r, u).wait_send()

        return carry

    lax.fori_loop(0, ntile, drain_parts, 0)

    for slot in range(max(LENT)):
        @pl.when(slot < taken)
        def _():
            pass_on(slot).wait_send()


def body(nctx, nhead, hidden_in, w_query, w_key, w_value, w_output, vertical, slash_offsets):
    rows, feat = hidden_in.shape
    hd = w_key.shape[1]
    qw = w_query.shape[1]
    width = w_output.shape[1]
    wide = qw + 2 * hd
    nchunk = rows // PIECE
    pairs = nhead // 2
    outer = nctx // 2
    out_rows = rows // nhead
    assert out_rows == BS and nhead % 2 == 0 and nctx % 2 == 0
    tn = 512 if width % 512 == 0 else 256
    ntile = width // tn
    vmem = pl.BlockSpec(memory_space=pltpu.VMEM)
    smem = pl.BlockSpec(memory_space=pltpu.SMEM)
    hbm = pl.BlockSpec(memory_space=pl.ANY)
    dma = pltpu.SemaphoreType.DMA
    return pl.pallas_call(
        functools.partial(kernel, nctx, nhead),
        out_shape=pltpu.VMEM((out_rows, width), BF16),
        in_specs=[smem, smem, hbm, hbm, hbm, hbm, hbm],
        out_specs=vmem,
        scratch_shapes=[
            pltpu.VMEM((nhead, feat, wide), BF16),
            pltpu.VMEM((qw, width), BF16),
            pltpu.VMEM((rows, feat), BF16),
            pltpu.VMEM((pairs - 1, nchunk, PIECE, feat), BF16),
            pltpu.VMEM((pairs - 1, nchunk, PIECE, feat), BF16),
            pltpu.VMEM((rows, wide), F32),
            pltpu.VMEM((rows, qw), BF16),
            pltpu.VMEM((nctx * nchunk, PIECE, 2 * hd), BF16),
            pltpu.VMEM((pairs, ntile, BS, tn), BF16),
            pltpu.VMEM((pairs - 1, 2 * ntile, BS, tn // 2), BF16),
            pltpu.VMEM((pairs, ntile, BS, tn), BF16),
            pltpu.VMEM((pairs - 1, 2 * ntile, BS, tn // 2), BF16),
            pltpu.VMEM((2, BS, qw), BF16),
            pltpu.VMEM((rows, hd), F32),
            pltpu.VMEM((rows, hd), F32),
            pltpu.VMEM((rows, feat), BF16),
            dma((5,)),
            dma((1,)), dma((1,)),
            dma((pairs - 1, nchunk)), dma((pairs - 1, nchunk)),
            dma((pairs - 1, nchunk)), dma((pairs - 1, nchunk)),
            dma((nchunk, outer)), dma((nchunk, outer)),
            dma((nchunk, outer)), dma((nchunk, outer)),
            dma((pairs, ntile)), dma((pairs, ntile)),
            dma((pairs - 1, 2 * ntile)), dma((pairs - 1, 2 * ntile)),
            pltpu.VMEM((max(LENT), BS, tn // 2), BF16),
            dma((max(LENT),)), dma((max(LENT),)), dma((max(LENT),)),
        ],
        compiler_params=pltpu.CompilerParams(
            collective_id=0, has_side_effects=True, vmem_limit_bytes=62 * 1024 * 1024
        ),
        name="layer",
    )(
        vertical[0], slash_offsets[0], hidden_in,
        w_query.reshape(nhead, feat, qw), w_key.reshape(nhead, feat, hd),
        w_value.reshape(nhead, feat, hd), w_output,
    )


def solution(mesh):
    placed = (
        P("ctx", "head"),
        P(None, "head"),
        P(None, "head"),
        P(None, "head"),
        P("head", None),
        P("head", None, None),
        P("head", None, None),
    )
    return jax.shard_map(
        functools.partial(body, mesh.shape["ctx"], mesh.shape["head"]),
        mesh=mesh, in_specs=placed, out_specs=P(("ctx", "head"), None), check_vma=False,
    )
```

```python
import functools
import math

import jax
import jax.numpy as jnp
from jax import lax
from jax.experimental import pallas as pl
from jax.experimental.pallas import tpu as pltpu
from jax.sharding import PartitionSpec as P

BS = 128
PIECE = 64
AHEAD = 1
LENT = (3, 1)
PASS_AT = 3
THETA = 10000000.0
MESH = pl.DeviceIdType.MESH
F32 = jnp.float32
BF16 = jnp.bfloat16


def rope_rates(head_dim):
    lane = lax.broadcasted_iota(jnp.int32, (1, head_dim), 1)
    j = jnp.where(lane < head_dim // 2, lane, lane - head_dim // 2).astype(F32)
    return jnp.exp(-(j * 2.0 / head_dim) * math.log(THETA))


def kernel(
    nctx, nhead,
    vert, slash, hid, wq, wk, wv, wo,
    out,
    w_s, wo_s, mate_x, far_x, fwd_x, acc, q_s, kv, part_m, part_x, in_m, in_x, ctx_s, cos, sin, hid_s,
    wsem, ms, mr, fs, fr, gs, gr, cs, cr, ys, yr, pms, pmr, pxs, pxr, lent_x, ls, lr, os,
):
    i, h = lax.axis_index("ctx"), lax.axis_index("head")
    o, p = i // 2, i % 2
    outer = nctx // 2
    pair, c0 = h // 2, h % 2
    pairs = nhead // 2
    hmate = h + 1 - 2 * c0
    ymate = i + 1 - 2 * p
    has_next, has_prev = o < outer - 1, o > 0
    rows = hid.shape[0]
    nchunk = rows // PIECE
    per = BS // PIECE
    hd = cos.shape[1]
    qh = q_s.shape[1] // hd
    ntile, tn = part_m.shape[1], part_m.shape[3]

    def far(d):
        return lax.rem(pair + d, pairs) * 2 + c0

    qw = wq.shape[2]
    loads = [
        pltpu.make_async_copy(wq, w_s.at[:, :, pl.ds(0, qw)], wsem.at[0]),
        pltpu.make_async_copy(wk, w_s.at[:, :, pl.ds(qw, hd)], wsem.at[1]),
        pltpu.make_async_copy(wv, w_s.at[:, :, pl.ds(qw + hd, hd)], wsem.at[2]),
        pltpu.make_async_copy(wo, wo_s, wsem.at[3]),
    ]
    own = pltpu.make_async_copy(hid, hid_s, wsem.at[4])
    own.start()
    for load in loads:
        load.start()

    barrier = pltpu.get_barrier_semaphore()

    def greet(where):
        pl.semaphore_signal(barrier, inc=1, device_id=where, device_id_type=MESH)

    greet({"head": hmate})
    for d in range(1, pairs):
        greet({"head": far(d)})
    greet({"ctx": ymate})

    @pl.when(has_next)
    def _():
        greet({"ctx": i + 2})

    @pl.when(has_prev)
    def _():
        greet({"ctx": i - 2})

    pl.semaphore_wait(
        barrier, pairs + 1 + jnp.where(has_next, 1, 0) + jnp.where(has_prev, 1, 0)
    )

    def remote(src, dst, send, recv, where):
        return pltpu.make_async_remote_copy(
            src_ref=src, dst_ref=dst, send_sem=send, recv_sem=recv,
            device_id=where, device_id_type=MESH,
        )

    def far_copy(d, c):
        return remote(
            hid.at[pl.ds(c * PIECE, PIECE), :], far_x.at[d - 1, c],
            fs.at[d - 1, c], fr.at[d - 1, c], {"head": far(d)},
        )

    def fwd_copy(d, c):
        return remote(
            far_x.at[d - 1, c], fwd_x.at[d - 1, c],
            gs.at[d - 1, c], gr.at[d - 1, c], {"head": hmate},
        )

    mate_copy = remote(hid, mate_x, ms.at[0], mr.at[0], {"head": hmate})
    for c in range(nchunk):
        for d in range(1, pairs):
            far_copy(d, c).start()
    mate_copy.start()

    def next_copy(c, so):
        block = kv.at[(so * 2 + p) * nchunk + c]
        return remote(block, block, cs.at[c, so], cr.at[c, so], {"ctx": i + 2})

    def side_copy(c, so, col):
        block = kv.at[(so * 2 + col) * nchunk + c]
        return remote(block, block, ys.at[c, so], yr.at[c, so], {"ctx": ymate})

    def relay(c, so):
        next_copy(c, so).wait_recv()

        @pl.when(has_next)
        def _():
            next_copy(c, so).start()

        side_copy(c, so, p).start()

    rates = rope_rates(hd)

    def table(c, carry):
        part = pl.ds(pl.multiple_of(c * PIECE, PIECE), PIECE)
        spot = lax.broadcasted_iota(jnp.int32, (PIECE, hd), 0) + (i * rows + c * PIECE)
        angle = spot.astype(F32) * rates
        lane = lax.broadcasted_iota(jnp.int32, (PIECE, hd), 1)
        sine = jnp.sin(angle)
        cos[part, :] = jnp.cos(angle)
        sin[part, :] = jnp.where(lane < hd // 2, -sine, sine)
        return carry

    lax.fori_loop(0, nchunk, table, 0)
    own.wait()
    for load in loads[:3]:
        load.wait()
    wide = w_s.shape[2]
    step = 256 if wide % 256 == 0 else 128

    def own_cols(t, carry):
        cols = pl.ds(pl.multiple_of(t * step, step), step)
        acc[:, cols] = jnp.dot(hid_s[...], w_s[h, :, cols], preferred_element_type=F32)
        return carry

    lax.fori_loop(0, wide // step, own_cols, 0)
    mate_copy.wait_recv()

    def mate_cols(t, carry):
        cols = pl.ds(pl.multiple_of(t * step, step), step)
        acc[:, cols] += jnp.dot(mate_x[...], w_s[hmate, :, cols], preferred_element_type=F32)
        return carry

    lax.fori_loop(0, wide // step, mate_cols, 0)

    def project(c):
        part = pl.ds(pl.multiple_of(c * PIECE, PIECE), PIECE)
        for d in range(1, pairs):
            far_copy(d, c).wait_recv()
            fwd_copy(d, c).start()
            src = lax.rem(pair + pairs - d, pairs) * 2
            acc[part, :] += jnp.dot(
                far_x[d - 1, c], w_s[src + c0], preferred_element_type=F32
            )
            fwd_copy(d, c).wait_recv()
            acc[part, :] += jnp.dot(
                fwd_x[d - 1, c], w_s[src + 1 - c0], preferred_element_type=F32
            )
        cosine, sine = cos[part, :], sin[part, :]

        def rope(u):
            return (u * cosine + pltpu.roll(u, hd // 2, 1) * sine).astype(BF16)

        mine = i * nchunk + c
        kv[mine, :, pl.ds(0, hd)] = rope(acc[part, pl.ds(qw, hd)])
        kv[mine, :, pl.ds(hd, hd)] = acc[part, pl.ds(qw + hd, hd)].astype(BF16)

        @pl.when(has_next)
        def _():
            next_copy(c, o).start()

        @pl.when(p == 0)
        def _():
            side_copy(c, o, p).start()

        for g in range(qh):
            q_s[part, pl.ds(g * hd, hd)] = rope(acc[part, pl.ds(g * hd, hd)])

    def turn(t, carry):
        @pl.when(t < nchunk)
        def _():
            project(t)

        for c in range(nchunk):
            s = t - c

            @pl.when((s >= 1) & (s <= o))
            def _():
                relay(c, o - s)

        return carry

    lax.fori_loop(0, nchunk + outer - 1, turn, 0)

    def passed(so, carry):
        for c in range(nchunk):
            side_copy(c, so, 1 - p).wait_recv()
        return carry

    lax.fori_loop(0, o + p, passed, 0)
    loads[3].wait()

    nv, ns = vert.shape[1], slash.shape[1]
    scale = 1.0 / math.sqrt(hd)
    below = lax.broadcasted_iota(jnp.int32, (BS, BS), 1) <= lax.broadcasted_iota(
        jnp.int32, (BS, BS), 0
    )
    low = F32(-1e30)

    def attend(b, into):
        qb = i * (rows // BS) + b
        query_rows = pl.ds(pl.multiple_of(b * BS, BS), BS)

        def held(at, lanes):
            return kv[pl.ds(at * per, per), :, lanes].reshape(BS, hd)

        for g in range(qh):
            slots = [qb]
            live = [None]
            for s in range(ns + nv):
                slot = qb - slash[g, s] if s < ns else vert[g, s - ns]
                ok = (slot >= 0) & (slot < qb)
                for earlier in slots[1:]:
                    ok = ok & (slot != earlier)
                slots.append(slot)
                live.append(ok)
            query = q_s[query_rows, pl.ds(g * hd, hd)]
            at = [s if ok is None else jnp.where(ok, s, qb) for s, ok in zip(slots, live)]
            groups = [[0]] + [[n, n + 1] for n in range(1, len(at) - 1, 2)]
            if len(at) % 2 == 0:
                groups.append([len(at) - 1])
            scores = []
            for group in groups:
                keys = jnp.concatenate([held(at[n], pl.ds(0, hd)) for n in group], axis=0)
                both = lax.dot_general(
                    query, keys, (((1,), (1,)), ((), ())), preferred_element_type=F32
                ) * F32(scale)
                for m, n in enumerate(group):
                    sc = both[:, m * BS:(m + 1) * BS]
                    scores.append(jnp.where(below if n == 0 else live[n], sc, low))
            top = functools.reduce(jnp.maximum, scores)
            top = jnp.max(top, axis=1, keepdims=True)
            total = None
            summed = None
            for group in groups:
                raws = [jnp.exp(scores[n] - top) for n in group]
                for raw in raws:
                    total = raw if total is None else total + raw
                vals = jnp.concatenate([held(at[n], pl.ds(hd, hd)) for n in group], axis=0)
                weights = jnp.concatenate([raw.astype(BF16) for raw in raws], axis=1)
                add = jnp.dot(weights, vals, preferred_element_type=F32)
                summed = add if summed is None else summed + add
            total = jnp.sum(total, axis=1, keepdims=True)
            ctx_s[into, :, pl.ds(g * hd, hd)] = (summed / total).astype(BF16)

    def share(t, of):
        cols = pl.ds(pl.multiple_of(t * tn, tn), tn)
        return jnp.dot(ctx_s[of], wo_s[:, cols], preferred_element_type=F32)

    def to_mate(r, t):
        return remote(
            part_m.at[r, t], in_m.at[r, t], pms.at[r, t], pmr.at[r, t], {"head": hmate}
        )

    helped = outer - 1 - o
    helps = o < outer // 2
    lends = o >= outer - outer // 2

    half = tn // 2

    def lent_by(q):
        return jnp.where(q >= outer - outer // 4, LENT[0], LENT[1])

    count = jnp.where(lends, lent_by(o), 0)
    taken = jnp.where(helps, lent_by(helped), 0)

    def to_far(r, u):
        return remote(
            part_x.at[r, u], in_x.at[r, u], pxs.at[r, u], pxr.at[r, u], {"head": far(r + 1)}
        )

    def is_lent(r, u):
        return (r == 0) & (u >= 4) & (u < 4 + count)

    def lend(u):
        return remote(
            part_x.at[0, u], lent_x.at[u - 4], ls.at[u - 4], lr.at[u - 4],
            {"ctx": helped * 2 + p, "head": far(1)},
        )

    def pass_on(slot):
        return remote(
            lent_x.at[slot], in_x.at[0, 4 + slot], os.at[slot], pxr.at[0, 4 + slot],
            {"ctx": helped * 2 + p},
        )

    def landed(slot):
        return remote(
            lent_x.at[slot], lent_x.at[slot], os.at[slot], lr.at[slot], {"head": far(1)},
        )

    def give(r, t):
        part_m[r, t] = share(t, 0).astype(BF16)
        to_mate(r, t).start()

    def round_of(r, carry):
        to = lax.rem(pair + r + 1, pairs) * 2
        attend(to + 1 - c0, 0)
        for t in range(AHEAD):
            give(r, t)
        attend(to + c0, 1)

        def tile(t, carry):
            mine = share(t, 1)
            to_mate(r, t).wait_recv()
            mine = (mine + in_m[r, t].astype(F32)).astype(BF16)
            for k in range(2):
                u = 2 * t + k
                part_x[r, u] = mine[:, k * half:(k + 1) * half]
                away = is_lent(r, u)

                @pl.when(away)
                def _():
                    lend(u).start()

                @pl.when(jnp.logical_not(away))
                def _():
                    to_far(r, u).start()

            @pl.when(t + AHEAD < ntile)
            def _():
                give(r, t + AHEAD)

            return carry

        lax.fori_loop(0, ntile, tile, 0)
        return carry

    lax.fori_loop(0, pairs - 1, round_of, 0)
    attend(pair * 2 + 1 - c0, 0)

    def give_last(t, carry):
        give(pairs - 1, t)
        return carry

    lax.fori_loop(0, ntile, give_last, 0)
    attend(h, 1)

    def last(t, carry):
        for slot in range(max(LENT)):
            @pl.when((t == min(PASS_AT, ntile - 1)) & (slot < taken))
            def _():
                landed(slot).wait_recv()
                pass_on(slot).start()

        mine = share(t, 1)
        to_mate(pairs - 1, t).wait_recv()
        mine = mine + in_m[pairs - 1, t].astype(F32)
        for k in range(2):
            u = 2 * t + k
            part = mine[:, k * half:(k + 1) * half]
            for r in range(pairs - 1):
                to_far(r, u).wait_recv()
                part = part + in_x[r, u].astype(F32)
            cols = pl.ds(pl.multiple_of(u * half, half), half)
            out[:, cols] = part.astype(out.dtype)
        return carry

    lax.fori_loop(0, ntile, last, 0)

    mate_copy.wait_send()
    for c in range(nchunk):
        for d in range(1, pairs):
            far_copy(d, c).wait_send()
            fwd_copy(d, c).wait_send()

    def drain_next(so, carry):
        for c in range(nchunk):
            next_copy(c, so).wait_send()
        return carry

    lax.fori_loop(0, jnp.where(has_next, o + 1, 0), drain_next, 0)

    def drain_side(so, carry):
        for c in range(nchunk):
            side_copy(c, so, p).wait_send()
        return carry

    lax.fori_loop(0, o + 1 - p, drain_side, 0)

    def drain_parts(t, carry):
        for r in range(pairs):
            to_mate(r, t).wait_send()
        for r in range(pairs - 1):
            for k in range(2):
                u = 2 * t + k
                away = is_lent(r, u)

                @pl.when(away)
                def _():
                    lend(u).wait_send()

                @pl.when(jnp.logical_not(away))
                def _():
                    to_far(r, u).wait_send()

        return carry

    lax.fori_loop(0, ntile, drain_parts, 0)

    for slot in range(max(LENT)):
        @pl.when(slot < taken)
        def _():
            pass_on(slot).wait_send()


def body(nctx, nhead, hidden_in, w_query, w_key, w_value, w_output, vertical, slash_offsets):
    rows, feat = hidden_in.shape
    hd = w_key.shape[1]
    qw = w_query.shape[1]
    width = w_output.shape[1]
    wide = qw + 2 * hd
    nchunk = rows // PIECE
    pairs = nhead // 2
    outer = nctx // 2
    out_rows = rows // nhead
    assert out_rows == BS and nhead % 2 == 0 and nctx % 2 == 0
    tn = 512 if width % 512 == 0 else 256
    ntile = width // tn
    vmem = pl.BlockSpec(memory_space=pltpu.VMEM)
    smem = pl.BlockSpec(memory_space=pltpu.SMEM)
    hbm = pl.BlockSpec(memory_space=pl.ANY)
    dma = pltpu.SemaphoreType.DMA
    return pl.pallas_call(
        functools.partial(kernel, nctx, nhead),
        out_shape=pltpu.VMEM((out_rows, width), BF16),
        in_specs=[smem, smem, hbm, hbm, hbm, hbm, hbm],
        out_specs=vmem,
        scratch_shapes=[
            pltpu.VMEM((nhead, feat, wide), BF16),
            pltpu.VMEM((qw, width), BF16),
            pltpu.VMEM((rows, feat), BF16),
            pltpu.VMEM((pairs - 1, nchunk, PIECE, feat), BF16),
            pltpu.VMEM((pairs - 1, nchunk, PIECE, feat), BF16),
            pltpu.VMEM((rows, wide), F32),
            pltpu.VMEM((rows, qw), BF16),
            pltpu.VMEM((nctx * nchunk, PIECE, 2 * hd), BF16),
            pltpu.VMEM((pairs, ntile, BS, tn), BF16),
            pltpu.VMEM((pairs - 1, 2 * ntile, BS, tn // 2), BF16),
            pltpu.VMEM((pairs, ntile, BS, tn), BF16),
            pltpu.VMEM((pairs - 1, 2 * ntile, BS, tn // 2), BF16),
            pltpu.VMEM((2, BS, qw), BF16),
            pltpu.VMEM((rows, hd), F32),
            pltpu.VMEM((rows, hd), F32),
            pltpu.VMEM((rows, feat), BF16),
            dma((5,)),
            dma((1,)), dma((1,)),
            dma((pairs - 1, nchunk)), dma((pairs - 1, nchunk)),
            dma((pairs - 1, nchunk)), dma((pairs - 1, nchunk)),
            dma((nchunk, outer)), dma((nchunk, outer)),
            dma((nchunk, outer)), dma((nchunk, outer)),
            dma((pairs, ntile)), dma((pairs, ntile)),
            dma((pairs - 1, 2 * ntile)), dma((pairs - 1, 2 * ntile)),
            pltpu.VMEM((max(LENT), BS, tn // 2), BF16),
            dma((max(LENT),)), dma((max(LENT),)), dma((max(LENT),)),
        ],
        compiler_params=pltpu.CompilerParams(
            collective_id=0, has_side_effects=True, vmem_limit_bytes=62 * 1024 * 1024
        ),
        name="layer",
    )(
        vertical[0], slash_offsets[0], hidden_in,
        w_query.reshape(nhead, feat, qw), w_key.reshape(nhead, feat, hd),
        w_value.reshape(nhead, feat, hd), w_output,
    )


def solution(mesh):
    placed = (
        P("ctx", "head"),
        P(None, "head"),
        P(None, "head"),
        P(None, "head"),
        P("head", None),
        P("head", None, None),
        P("head", None, None),
    )
    return jax.shard_map(
        functools.partial(body, mesh.shape["ctx"], mesh.shape["head"]),
        mesh=mesh, in_specs=placed, out_specs=P(("ctx", "head"), None), check_vma=False,
    )
```
